32 devices in a mesh: owner: 16 (over z, x, core), dense: 2 (over y).
Axes of the slice: x: 2, y: 2, z: 4, core: 2. Of those that a mesh axis runs over, the one named last changes fastest.
Arguments:
- owners: int32 [8192, 13, 4], P(('owner', 'dense')), may hold values from 0 to 15, all different within a row; in each aligned block of 3328 rows (0 to 3327, 3328 to 6655, ..., all dimensions but the last counted through in order) at most 1664 rows name the same one
- local_rows: int32 [8192, 13, 4], P(('owner', 'dense')), may hold values from 0 to 2047, as said below
- weights: float32 [8192, 13, 4], P(('owner', 'dense')), may hold values from 0.25 to 4
- labels: bfloat16 [8192], P(('owner', 'dense')), may hold values from 0 to 1
- table: float32 [32768, 128], P('owner'), may hold values from -6 to 6
- accum: float32 [32768], P('owner'), may hold values from 0.0001 to 0.01
- w_in: bfloat16 [1664, 4096], P(None, 'dense'), may hold values from -0.15625 to 0.15625
- b_in: bfloat16 [4096], P('dense'), may hold values from -3 to 3
- w_out: bfloat16 [4096], P('dense'), may hold values from -0.29882812 to 0.29882812
Outputs:
- new_table: float32 [32768, 128], P('owner')
- new_accum: float32 [32768], P('owner')
- weight_grad: float32 [8192, 13, 4], P(('owner', 'dense'))
The draws below stay inside these ranges and needn't reach their ends.
Inputs may be any that keep to these rules, and one draw needn't show every extreme that they name: The 4 owners of one bag differ. Among the bags of one device (3328 of them, aligned blocks of rows), at most 1664 name one owner. Among the ids of one device's samples (13312 of them, aligned blocks of rows), exactly 416 distinct values of local_rows occur.
All inputs are finite; a program needn't handle non-finite values.
Results may differ from the reference program's by a relative error of at most 0.0056.
Values may be sent and summed in bfloat16 or wider, within the bound.
A program may use at most 128 MiB of HBM per device.

```python
import math
import jax
import jax.numpy as jnp
import numpy as np
from jax import lax

E = 128
F = 13
L = 4
H = 4096
S_DEV = 256
ROWS_DEV = 2048
CAP = 1664
UNIQ = 416
SAMPLES = 8192
ROWS = 32768
N_OWNER = 16


def draw_local_rows(key, part):
    device_count = SAMPLES // S_DEV
    per_device = S_DEV * F * L

    def one_device(dev_key):
        pool_key, first_key, second_key = jax.random.split(dev_key, 3)
        pool = jax.random.permutation(pool_key, ROWS_DEV)[:UNIQ]
        first_pick = jax.random.randint(first_key, (per_device,), 0, UNIQ)
        second_pick = jax.random.randint(second_key, (per_device,), 0, UNIQ)
        picked = jnp.minimum(first_pick, second_pick)
        picked = picked.at[:UNIQ].set(jnp.arange(UNIQ, dtype=picked.dtype))
        return pool[picked]
    dev_keys = jax.random.split(jax.random.fold_in(key, 71), device_count)
    return jax.vmap(one_device)(dev_keys).reshape(SAMPLES, F, L).astype(jnp.int32)


def shard_levels(own_key, shape, cuts, smallest, high):
    factor_of = 1.0
    for axis_at, shards_of in cuts:
        heights = jax.random.uniform(jax.random.fold_in(jax.random.fold_in(own_key, 6), axis_at), (shards_of,), jnp.float32, smallest / len(cuts), high / len(cuts))
        factor_of = factor_of * jnp.repeat(jnp.exp(heights), shape[axis_at] // shards_of).reshape((-1,) + (1,) * (len(shape) - 1 - axis_at))
    return factor_of


def deal_out(own_key, own, number, rows, amount, top, bound, lean):
    order = jax.random.permutation(own_key, amount)
    heavy_load, usual = load_shares(amount, rows * top, bound, lean, True), load_shares(amount, rows * top, bound, lean, False)
    places = jnp.arange(amount)

    def named(tallies, offset_by):
        used = int((tallies > 0).sum())
        fixed = max(1, used // 4)
        shifted = fixed + (places - fixed + offset_by * (used - fixed)) % max(1, amount - fixed)
        return jnp.zeros((amount,), jnp.int32).at[order[jnp.where(places < fixed, places, shifted)]].set(jnp.asarray(tallies, jnp.int32))

    tallies = jnp.where(number % 4 == 0, named(heavy_load, number // 4), named(usual, number - number // 4 - 1))
    mixed = jax.random.permutation(jax.random.fold_in(own, 3), amount)
    source_of, taker = mixed[0:amount // 2 * 2:2], mixed[1:amount // 2 * 2:2]
    slack = jnp.minimum(tallies[source_of] - 1, bound - tallies[taker]) // 2
    slack = jnp.where((source_of == order[0]) | (taker == order[0]) | (tallies[taker] == 0), 0, jnp.maximum(slack, 0))
    shifted = jax.random.randint(jax.random.fold_in(own, 4), (amount // 2,), 0, 1 << 20) % (slack + 1)
    tallies = tallies.at[source_of].add(-shifted).at[taker].add(shifted)
    items = jnp.searchsorted(jnp.cumsum(tallies), jnp.arange(rows * top), side="right").astype(jnp.int32)
    grid = items.reshape(top, rows).T
    grid = grid[jax.random.permutation(jax.random.fold_in(own, 1), rows)]
    offset_by = jax.random.randint(jax.random.fold_in(own, 2), (rows, 1), 0, top)
    return jnp.take_along_axis(grid, (jnp.arange(top)[None, :] + offset_by) % top, axis=1)


def load_shares(amount, total, reach, lean, full):
    portions = [(1 << 20) // math.isqrt(rank ** lean) + 1 for rank in range(1, amount + 1)]
    largest = reach if full else min(reach, max(-(-total // amount), total * portions[0] // sum(portions)))
    least = 1 if total - largest >= amount - 1 else 0
    holding, spare = [largest] + [least] * (amount - 1), total - largest - least * (amount - 1)
    while spare > 0:
        free = [i for i in range(1, amount) if holding[i] < largest] or [i for i in range(1, amount) if holding[i] < reach]
        whole, budget = sum([portions[i] for i in free]), spare
        for i in free:
            addition = min(reach - holding[i], max(1, budget * portions[i] // whole), spare)
            holding[i] = holding[i] + addition
            spare = spare - addition
    return np.array(holding)


def centred(stream_key, shape, width, bound, cuts=(), kind=jnp.bfloat16):
    gain = shard_levels(stream_key, shape, cuts, -0.22, 0.18) if cuts else 1.0
    values = jax.random.normal(stream_key, shape, jnp.float32) * width * gain
    return jnp.minimum(jnp.maximum(values, -bound), bound).astype(kind)


def setup_inputs(seed: int = 0) -> dict:
    seeds = jax.random.split(jax.random.key(seed), 10)
    owners_keys = jax.random.split(jax.random.fold_in(seeds[0], 1), SAMPLES * F // (S_DEV * F))
    owners_turns = jax.random.permutation(jax.random.fold_in(seeds[0], 3), SAMPLES * F // (S_DEV * F))
    owners = jax.vmap(lambda own, number: deal_out(jax.random.fold_in(seeds[0], 2), own, number, S_DEV * F, N_OWNER, L, CAP, 2))(owners_keys, owners_turns).reshape((SAMPLES, F, L))
    local_rows = draw_local_rows(jax.random.fold_in(seeds[9], 71), 0)
    weights = jnp.clip(jnp.exp(math.log(4.0) - 2.7725887 * jax.random.uniform(seeds[2], (SAMPLES, F, L), jnp.float32) ** shard_levels(seeds[2], (SAMPLES, F, L), ((0, 32),), -0.2, 0.2)), 0.25, 4.0)
    labels = jnp.clip(1.0 * jax.random.uniform(seeds[3], (SAMPLES,), jnp.float32) ** shard_levels(seeds[3], (SAMPLES,), ((0, 32),), -0.2, 0.2), 0.0, 1.0).astype(jnp.bfloat16)
    table = centred(seeds[4], (ROWS, E), 1.0, 6.0, ((0, 16),), jnp.float32)
    accum = jnp.clip(jnp.exp(math.log(0.01) - 4.6051702 * jax.random.uniform(seeds[5], (ROWS,), jnp.float32) ** shard_levels(seeds[5], (ROWS,), ((0, 16),), -0.2, 0.2)), 0.0001, 0.01)
    w_in = centred(seeds[6], (F * E, H), (F * E) ** -0.5, 0.15625, ((1, 2),))
    b_in = centred(seeds[7], (H,), 0.5, 3.0, ((0, 2),))
    w_out = centred(seeds[8], (H,), 0.05, 0.29882812, ((0, 2),))
    return dict(owners=owners, local_rows=local_rows, weights=weights, labels=labels, table=table, accum=accum, w_in=w_in, b_in=b_in, w_out=w_out)


step_size = 0.5

def reference(owners, local_rows, weights, labels, table, accum, w_in, b_in, w_out):
    block_rows = math.gcd(SAMPLES, 1024)
    block_count = SAMPLES // block_rows
    row_ids = (owners * ROWS_DEV + local_rows).astype(jnp.int32)
    bias = b_in.astype(jnp.float32)
    out_proj = w_out.astype(jnp.float32)

    def accumulate(row_grad, blocks):
        block_ids, bag_weights, bag_labels = blocks
        looked = table[block_ids].astype(jnp.bfloat16)
        looked_f = looked.astype(jnp.float32)
        weight_sums = lax.optimization_barrier(jnp.sum(bag_weights, axis=-1))
        pooled = lax.optimization_barrier(jnp.sum(bag_weights[..., None] * looked_f, axis=2)) / weight_sums[..., None]
        inputs = pooled.astype(jnp.bfloat16).reshape(block_rows, F * E)
        preact = jnp.dot(inputs, w_in, preferred_element_type=jnp.float32) + bias
        sigma_pre = jax.nn.sigmoid(preact)
        logits = lax.optimization_barrier(jnp.sum(preact * sigma_pre * out_proj, axis=-1))
        logit_grad = jax.nn.sigmoid(logits) - bag_labels.astype(jnp.float32)
        slope = sigma_pre * (1.0 + preact * (1.0 - sigma_pre))
        dhidden = (logit_grad[:, None] * out_proj * slope).astype(jnp.bfloat16)
        dinputs = lax.dot_general(dhidden, w_in, (((1,), (1,)), ((), ())), preferred_element_type=jnp.float32)
        dpooled = dinputs.reshape(block_rows, F, E)
        along = lax.optimization_barrier(jnp.sum(looked_f * dpooled[:, :, None, :], axis=-1))
        centre = lax.optimization_barrier(jnp.sum(pooled * dpooled, axis=-1))
        weight_grads = (along - centre[..., None]) / weight_sums[..., None]
        slot_grad = ((bag_weights / weight_sums[..., None])[..., None] * dpooled[:, :, None, :]).astype(jnp.bfloat16)
        row_grad = row_grad.at[block_ids.reshape(-1)].add(slot_grad.reshape(-1, E).astype(jnp.float32))
        return (row_grad, weight_grads)
    start_grad = jnp.zeros((ROWS_DEV * N_OWNER, E), jnp.float32)
    row_grad, weight_grads = lax.scan(accumulate, start_grad, (row_ids.reshape(block_count, block_rows, F, L), weights.reshape(block_count, block_rows, F, L), labels.reshape(block_count, block_rows)))
    new_accum = accum + lax.optimization_barrier(jnp.mean(row_grad * row_grad, axis=-1))
    new_table = table - step_size * row_grad / jnp.sqrt(new_accum)[:, None]
    return (new_table, new_accum, weight_grads.reshape(SAMPLES, F, L))
```

```python
import functools

import jax
import jax.numpy as jnp
from jax import lax
from jax.experimental import pallas as pl
from jax.experimental.pallas import tpu as pltpu
from jax.sharding import PartitionSpec as P

step_size = 0.5
lane = 128
f32 = jnp.float32
bf16 = jnp.bfloat16


def vmem():
    return pl.BlockSpec(memory_space=pltpu.VMEM)


def distinct_body(table_rows, own_ref, loc_ref, w_ref, uniq_ref, lo_ref, wo_ref):
    bag_len, bags = own_ref.shape
    groups = lo_ref.shape[0]
    uniq = uniq_ref.shape[0]
    highs = table_rows // lane
    counts = jnp.zeros((highs, lane), f32)
    owner_at = lax.broadcasted_iota(jnp.int32, (groups, bags), 0)
    low_at = lax.broadcasted_iota(jnp.int32, (lane, bags), 0)
    high_at = lax.broadcasted_iota(jnp.int32, (highs, bags), 0)
    named = jnp.full((groups, bags), -1, jnp.int32)
    weight = jnp.zeros((groups, bags), f32)
    for slot in range(bag_len):
        loc = loc_ref[slot : slot + 1, :]
        hit = own_ref[slot : slot + 1, :] == owner_at
        named = jnp.where(hit, loc, named)
        weight = jnp.where(hit, w_ref[slot : slot + 1, :], weight)
        low = jnp.where(jnp.bitwise_and(loc, lane - 1) == low_at, 1.0, 0.0).astype(bf16)
        high = jnp.where(jnp.right_shift(loc, 7) == high_at, 1.0, 0.0).astype(bf16)
        counts += lax.dot_general(high, low, (((1,), (1,)), ((), ())), preferred_element_type=f32)
    lo_ref[...] = named
    wo_ref[...] = weight
    present = jnp.where(counts > 0.0, 1.0, 0.0)
    upper = jnp.where(
        lax.broadcasted_iota(jnp.int32, (lane, lane), 0)
        <= lax.broadcasted_iota(jnp.int32, (lane, lane), 1),
        1.0,
        0.0,
    ).astype(bf16)
    inclusive = jnp.dot(present.astype(bf16), upper, preferred_element_type=f32)
    place = lax.broadcasted_iota(jnp.int32, (uniq, lane), 0).astype(f32)
    lane_at = lax.broadcasted_iota(jnp.int32, (1, lane), 1).astype(f32)
    before = jnp.zeros((1, 1), f32)
    found = jnp.zeros((uniq, lane), f32)
    for h in range(highs):
        here = present[h : h + 1, :]
        rank = jnp.where(here > 0.0, inclusive[h : h + 1, :] + before - 1.0, -1.0)
        found += jnp.where(place == rank, lane_at + float(h * lane), 0.0)
        before += jnp.sum(here, axis=1, keepdims=True)
    uniq_ref[...] = jnp.sum(found, axis=1, keepdims=True).astype(jnp.int32)


def lookup_body(list_ref, table_ref, out_ref):
    uniq = list_ref.shape[1]
    rows = table_ref.shape[0]
    at = lax.broadcasted_iota(jnp.int32, (uniq, rows), 1)
    pick = jnp.where(list_ref[0] == at, 1.0, 0.0).astype(bf16)
    out_ref[0] = jnp.dot(pick, table_ref[...], preferred_element_type=f32).astype(bf16)


def pool_body(uniq_ref, rows_ref, lo_ref, wo_ref, out_ref):
    groups = rows_ref.shape[0]
    named = lo_ref[...].T
    weight = wo_ref[...].T
    total = jnp.sum(weight, axis=1, keepdims=True)
    distinct = uniq_ref[...]
    acc = jnp.zeros(out_ref.shape, f32)
    for o in range(groups):
        mix = jnp.where(named[:, o : o + 1] == distinct, weight[:, o : o + 1], 0.0).astype(bf16)
        acc += jnp.dot(mix, rows_ref[o], preferred_element_type=f32)
    out_ref[...] = (acc / total).astype(bf16)


def backward_body(
    uniq_ref, rows_ref, lo_ref, wo_ref, own_ref, w_ref, dp_ref, grad_ref, wg_ref, acc, wide
):
    groups = rows_ref.shape[0]
    f = pl.program_id(0)

    @pl.when(f == 0)
    def _():
        acc[...] = jnp.zeros_like(acc)
        wide[...] = jnp.broadcast_to(uniq_ref[...], wide.shape)

    dp = dp_ref[...]
    dp_rows = dp.astype(bf16)
    dp_cols = dp.T.astype(bf16)
    slot_w = w_ref[...]
    own = own_ref[...]
    total = jnp.sum(slot_w, axis=0, keepdims=True)
    scaled = wo_ref[...] / total
    along = jnp.zeros(slot_w.shape, f32)
    for o in range(groups):
        hit = wide[...] == lo_ref[o : o + 1, :]
        mix = jnp.where(hit, scaled[o : o + 1, :], 0.0).astype(bf16)
        acc[o] += jnp.dot(mix, dp_rows, preferred_element_type=f32)
        dots = jnp.dot(rows_ref[o], dp_cols, preferred_element_type=f32)
        mine = jnp.sum(jnp.where(hit, dots, 0.0), axis=0, keepdims=True)
        along += jnp.where(own == o, mine, 0.0)
    centre = jnp.sum(slot_w * along, axis=0, keepdims=True) / total
    wg_ref[...] = (along - centre) / total

    @pl.when(f == pl.num_programs(0) - 1)
    def _():
        grad_ref[...] = acc[...].astype(bf16)


def collect_body(list_ref, got_ref, out_ref):
    groups, uniq = list_ref.shape
    rows = out_ref.shape[0]
    at = lax.broadcasted_iota(jnp.int32, (rows, uniq), 0) + pl.program_id(0) * rows
    acc = jnp.zeros(out_ref.shape, f32)
    for q in range(groups):
        pick = jnp.where(list_ref[q : q + 1, :] == at, 1.0, 0.0).astype(bf16)
        acc += jnp.dot(pick, got_ref[q], preferred_element_type=f32)
    out_ref[...] = acc.astype(bf16)


def head_pieces(w_in, b_in, w_out):
    groups = lax.axis_size("owner")
    parts = lax.axis_size("dense")
    half = w_in.shape[1] // 2
    core = lax.rem(lax.axis_index("owner"), 2)
    pieces = [(w_in, b_in, w_out)]
    mine = lax.dynamic_slice_in_dim(w_in, core * half, half, axis=1)
    swap = [(g, g + 1 - 2 * (g % 2)) for g in range(groups)]
    for shift in range(1, parts):
        ring = [(d, (d + shift) % parts) for d in range(parts)]
        w_here = lax.ppermute(mine, "dense", ring)
        b_all = lax.ppermute(b_in, "dense", ring)
        o_all = lax.ppermute(w_out, "dense", ring)
        w_there = lax.ppermute(w_here, "owner", swap)
        for w_piece, at in ((w_here, core * half), (w_there, (1 - core) * half)):
            pieces.append(
                (
                    w_piece,
                    lax.dynamic_slice_in_dim(b_all, at, half),
                    lax.dynamic_slice_in_dim(o_all, at, half),
                )
            )
    return pieces


def head(inputs, labels, pieces):
    kept = []
    logits = jnp.zeros((inputs.shape[0],), f32)
    for w, b, out in pieces:
        out = out.astype(f32)
        preact = jnp.dot(inputs, w, preferred_element_type=f32) + b.astype(f32)
        sigma = jax.nn.sigmoid(preact)
        logits += jnp.sum(preact * sigma * out, axis=-1)
        kept.append((w, out, preact, sigma))
    logit_grad = jax.nn.sigmoid(logits) - labels.astype(f32)
    dinputs = None
    for w, out, preact, sigma in kept:
        slope = sigma * (1.0 + preact * (1.0 - sigma))
        dhidden = (logit_grad[:, None] * out * slope).astype(bf16)
        term = lax.dot_general(dhidden, w, (((1,), (1,)), ((), ())), preferred_element_type=f32)
        dinputs = term if dinputs is None else dinputs + term
    return dinputs


def local(owners, local_rows, weights, labels, table, accum, w_in, b_in, w_out):
    samples, fields, bag_len = owners.shape
    table_rows, width = table.shape
    groups = lax.axis_size("owner")
    parts = lax.axis_size("dense")
    bags = samples * fields
    uniq = bags * bag_len // (2 * groups)
    pieces = head_pieces(w_in, b_in, w_out)

    def by_slot(x):
        return x.transpose(2, 1, 0).reshape(bag_len, bags)

    own, loc, w = by_slot(owners), by_slot(local_rows), by_slot(weights)
    distinct, named, spread = pl.pallas_call(
        functools.partial(distinct_body, table_rows),
        out_shape=(
            jax.ShapeDtypeStruct((uniq, 1), jnp.int32),
            jax.ShapeDtypeStruct((groups, bags), jnp.int32),
            jax.ShapeDtypeStruct((groups, bags), f32),
        ),
        in_specs=[vmem()] * 3,
        out_specs=(vmem(),) * 3,
        name="distinct",
    )(own, loc, w)
    distinct_row = distinct.reshape(1, uniq)
    lists = lax.all_gather(distinct_row, "owner", axis=0, tiled=True)
    found = pl.pallas_call(
        lookup_body,
        grid=(groups,),
        out_shape=jax.ShapeDtypeStruct((groups, uniq, width), bf16),
        in_specs=[pl.BlockSpec((1, uniq, 1), lambda q: (q, 0, 0)), vmem()],
        out_specs=pl.BlockSpec((1, uniq, width), lambda q: (q, 0, 0)),
        name="lookup",
    )(lists[:, :, None], table.astype(bf16))
    rows = lax.all_to_all(found, "owner", split_axis=0, concat_axis=0, tiled=True)

    block = pl.BlockSpec((groups, samples), lambda f: (0, f))
    slots = pl.BlockSpec((bag_len, samples), lambda f: (0, f))
    field = pl.BlockSpec((samples, width), lambda f: (0, f))
    inputs = pl.pallas_call(
        pool_body,
        grid=(fields,),
        out_shape=jax.ShapeDtypeStruct((samples, fields * width), bf16),
        in_specs=[vmem(), vmem(), block, block],
        out_specs=field,
        name="pool",
    )(distinct_row, rows, named, spread)

    dinputs = head(inputs, labels, pieces)

    grads, weight_grad = pl.pallas_call(
        backward_body,
        grid=(fields,),
        out_shape=(
            jax.ShapeDtypeStruct((groups, uniq, width), bf16),
            jax.ShapeDtypeStruct((bag_len, bags), f32),
        ),
        in_specs=[vmem(), vmem(), block, block, slots, slots, field],
        out_specs=(vmem(), slots),
        scratch_shapes=[
            pltpu.VMEM((groups, uniq, width), f32),
            pltpu.VMEM((uniq, samples), jnp.int32),
        ],
        name="backward",
    )(distinct, rows, named, spread, own, w, dinputs)
    weight_grad = weight_grad.reshape(bag_len, fields, samples).transpose(2, 1, 0)

    got = lax.all_to_all(grads, "owner", split_axis=0, concat_axis=0, tiled=True)
    chunk = table_rows // 8
    row_part = pl.pallas_call(
        collect_body,
        grid=(table_rows // chunk,),
        out_shape=jax.ShapeDtypeStruct((table_rows, width), bf16),
        in_specs=[vmem(), vmem()],
        out_specs=pl.BlockSpec((chunk, width), lambda r: (r, 0)),
        name="collect",
    )(lists, got)
    if parts == 2:
        other = lax.ppermute(row_part, "dense", [(0, 1), (1, 0)])
        row_grad = row_part.astype(f32) + other.astype(f32)
    else:
        row_grad = lax.psum(row_part, "dense").astype(f32)
    new_accum = accum + jnp.mean(row_grad * row_grad, axis=-1)
    new_table = table - step_size * row_grad / jnp.sqrt(new_accum)[:, None]
    return (new_table, new_accum, weight_grad)


def solution(mesh):
    placed = (
        P(("owner", "dense"), None, None),
        P(("owner", "dense"), None, None),
        P(("owner", "dense"), None, None),
        P(("owner", "dense")),
        P("owner", None),
        P("owner"),
        P(None, "dense"),
        P("dense"),
        P("dense"),
    )
    return jax.shard_map(
        local,
        mesh=mesh,
        in_specs=placed,
        out_specs=(P("owner", None), P("owner"), P(("owner", "dense"), None, None)),
        check_vma=False,
    )
```

```python
import functools

import jax
import jax.numpy as jnp
from jax import lax
from jax.experimental import pallas as pl
from jax.experimental.pallas import tpu as pltpu
from jax.sharding import PartitionSpec as P

step_size = 0.5
lane = 128
f32 = jnp.float32
bf16 = jnp.bfloat16


def vmem():
    return pl.BlockSpec(memory_space=pltpu.VMEM)


def distinct_body(table_rows, own_ref, loc_ref, w_ref, uniq_ref, row_ref, lo_ref, wo_ref):
    bag_len, bags = own_ref.shape
    groups = lo_ref.shape[0]
    uniq = uniq_ref.shape[0]
    padded = row_ref.shape[1]
    highs = table_rows // lane
    counts = jnp.zeros((highs, lane), f32)
    owner_at = lax.broadcasted_iota(jnp.int32, (groups, bags), 0)
    low_at = lax.broadcasted_iota(jnp.int32, (lane, bags), 0)
    high_at = lax.broadcasted_iota(jnp.int32, (highs, bags), 0)
    named = jnp.full((groups, bags), -1, jnp.int32)
    weight = jnp.zeros((groups, bags), f32)
    for slot in range(bag_len):
        loc = loc_ref[slot : slot + 1, :]
        hit = own_ref[slot : slot + 1, :] == owner_at
        named = jnp.where(hit, loc, named)
        weight = jnp.where(hit, w_ref[slot : slot + 1, :], weight)
        low = jnp.where(jnp.bitwise_and(loc, lane - 1) == low_at, 1.0, 0.0).astype(bf16)
        high = jnp.where(jnp.right_shift(loc, 7) == high_at, 1.0, 0.0).astype(bf16)
        counts += lax.dot_general(high, low, (((1,), (1,)), ((), ())), preferred_element_type=f32)
    lo_ref[...] = named
    wo_ref[...] = weight
    present = jnp.where(counts > 0.0, 1.0, 0.0)
    upper = jnp.where(
        lax.broadcasted_iota(jnp.int32, (lane, lane), 0)
        <= lax.broadcasted_iota(jnp.int32, (lane, lane), 1),
        1.0,
        0.0,
    ).astype(bf16)
    inclusive = jnp.dot(present.astype(bf16), upper, preferred_element_type=f32)
    place = lax.broadcasted_iota(jnp.int32, (padded, lane), 0).astype(f32)
    lane_at = lax.broadcasted_iota(jnp.int32, (1, lane), 1).astype(f32)
    before = jnp.zeros((1, 1), f32)
    found = jnp.where(place < float(uniq), 0.0, -1.0)
    for h in range(highs):
        here = present[h : h + 1, :]
        rank = jnp.where(here > 0.0, inclusive[h : h + 1, :] + before - 1.0, -1.0)
        found += jnp.where(place == rank, lane_at + float(h * lane), 0.0)
        before += jnp.sum(here, axis=1, keepdims=True)
    column = jnp.sum(found, axis=1, keepdims=True)
    uniq_ref[...] = column[:uniq].astype(jnp.int32)
    row_ref[...] = jnp.broadcast_to(column, (padded, lane)).T[0:1].astype(jnp.int32)


def share_body(groups, row_ref, out_ref, send_sem, recv_sem, own_sem):
    me = lax.axis_index("owner")
    barrier = pltpu.get_barrier_semaphore()
    for k in range(1, groups):
        peer = lax.rem(me + k, groups)
        pl.semaphore_signal(
            barrier, inc=1, device_id={"owner": peer}, device_id_type=pl.DeviceIdType.MESH
        )
    pl.semaphore_wait(barrier, groups - 1)
    copies = []
    for k in range(1, groups):
        copies.append(
            pltpu.make_async_remote_copy(
                src_ref=row_ref,
                dst_ref=out_ref.at[me],
                send_sem=send_sem.at[k],
                recv_sem=recv_sem.at[k],
                device_id={"owner": lax.rem(me + k, groups)},
                device_id_type=pl.DeviceIdType.MESH,
            )
        )
    for copy in copies:
        copy.start()
    mine = pltpu.make_async_copy(row_ref, out_ref.at[me], own_sem)
    mine.start()
    mine.wait()
    for copy in copies:
        copy.wait()


def lookup_body(list_ref, table_ref, out_ref, wide, columns):
    groups, uniq, width = out_ref.shape
    depth = wide.shape[0]
    folds = table_ref.shape[0] // depth
    for j in range(folds):
        wide[:, j * width : (j + 1) * width] = table_ref[j * depth : (j + 1) * depth, :].astype(bf16)
    columns[...] = list_ref[...].T
    at = lax.broadcasted_iota(jnp.int32, (uniq, depth), 1)
    for q in range(groups):
        ids = columns[:uniq, q : q + 1]
        fold = ids // depth
        pick = jnp.where(ids - fold * depth == at, 1.0, 0.0).astype(bf16)
        every = jnp.dot(pick, wide[...], preferred_element_type=f32)
        row = every[:, :width]
        for j in range(1, folds):
            row = jnp.where(fold == j, every[:, j * width : (j + 1) * width], row)
        out_ref[q] = row.astype(bf16)


def pool_body(uniq_ref, rows_ref, lo_ref, wo_ref, out_ref):
    groups = rows_ref.shape[0]
    named = lo_ref[...].T
    weight = wo_ref[...].T
    total = jnp.sum(weight, axis=1, keepdims=True)
    distinct = uniq_ref[...]
    acc = jnp.zeros(out_ref.shape, f32)
    for o in range(groups):
        mix = jnp.where(named[:, o : o + 1] == distinct, weight[:, o : o + 1], 0.0).astype(bf16)
        acc += jnp.dot(mix, rows_ref[o], preferred_element_type=f32)
    out_ref[...] = (acc / total).astype(bf16)


def backward_body(
    uniq_ref, rows_ref, lo_ref, wo_ref, own_ref, w_ref, dp_ref, grad_ref, wg_ref, acc, wide
):
    groups = rows_ref.shape[0]
    f = pl.program_id(0)

    @pl.when(f == 0)
    def _():
        acc[...] = jnp.zeros_like(acc)
        wide[...] = jnp.broadcast_to(uniq_ref[...], wide.shape)

    dp = dp_ref[...]
    dp_rows = dp.astype(bf16)
    dp_cols = dp.T.astype(bf16)
    slot_w = w_ref[...]
    own = own_ref[...]
    total = jnp.sum(slot_w, axis=0, keepdims=True)
    scaled = wo_ref[...] / total
    along = jnp.zeros(slot_w.shape, f32)
    for o in range(groups):
        hit = wide[...] == lo_ref[o : o + 1, :]
        mix = jnp.where(hit, scaled[o : o + 1, :], 0.0).astype(bf16)
        acc[o] += jnp.dot(mix, dp_rows, preferred_element_type=f32)
        dots = jnp.dot(rows_ref[o], dp_cols, preferred_element_type=f32)
        mine = jnp.sum(jnp.where(hit, dots, 0.0), axis=0, keepdims=True)
        along += jnp.where(own == o, mine, 0.0)
    centre = jnp.sum(slot_w * along, axis=0, keepdims=True) / total
    wg_ref[...] = (along - centre) / total

    @pl.when(f == pl.num_programs(0) - 1)
    def _():
        grad_ref[...] = acc[...].astype(bf16)


def collect_body(base, list_ref, got_ref, out_ref, columns, acc):
    groups, uniq, width = got_ref.shape
    half = out_ref.shape[0] // 2
    columns[...] = list_ref[...].T - base
    at = lax.broadcasted_iota(jnp.int32, (half, uniq), 0)
    for q in range(groups):
        row = list_ref[q : q + 1, :uniq] - base
        row = jnp.where(row >= half, row - half, row)
        pick = jnp.where(row == at, 1.0, 0.0).astype(bf16)
        ids = columns[:uniq, q : q + 1]
        got = got_ref[q].astype(f32)
        first = jnp.where(ids < half, got, 0.0)
        second = jnp.where(ids >= half, got, 0.0)
        both = jnp.concatenate([first, second], axis=1).astype(bf16)
        term = jnp.dot(pick, both, preferred_element_type=f32)
        if q == 0:
            acc[...] = term
        else:
            acc[...] += term
    out_ref[:half] = acc[:, :width].astype(bf16)
    out_ref[half:] = acc[:, width:].astype(bf16)


def head_pieces(w_in, b_in, w_out):
    groups = lax.axis_size("owner")
    parts = lax.axis_size("dense")
    half = w_in.shape[1] // 2
    core = lax.rem(lax.axis_index("owner"), 2)
    pieces = [(w_in, b_in, w_out)]
    mine = lax.dynamic_slice_in_dim(w_in, core * half, half, axis=1)
    swap = [(g, g + 1 - 2 * (g % 2)) for g in range(groups)]
    for shift in range(1, parts):
        ring = [(d, (d + shift) % parts) for d in range(parts)]
        w_here = lax.ppermute(mine, "dense", ring)
        b_all = lax.ppermute(b_in, "dense", ring)
        o_all = lax.ppermute(w_out, "dense", ring)
        w_there = lax.ppermute(w_here, "owner", swap)
        for w_piece, at in ((w_here, core * half), (w_there, (1 - core) * half)):
            pieces.append(
                (
                    w_piece,
                    lax.dynamic_slice_in_dim(b_all, at, half),
                    lax.dynamic_slice_in_dim(o_all, at, half),
                )
            )
    return pieces


def head(inputs, labels, pieces):
    kept = []
    logits = jnp.zeros((inputs.shape[0],), f32)
    for w, b, out in pieces:
        out = out.astype(f32)
        preact = jnp.dot(inputs, w, preferred_element_type=f32) + b.astype(f32)
        sigma = jax.nn.sigmoid(preact)
        logits += jnp.sum(preact * sigma * out, axis=-1)
        kept.append((w, out, preact, sigma))
    logit_grad = jax.nn.sigmoid(logits) - labels.astype(f32)
    dinputs = None
    for w, out, preact, sigma in kept:
        slope = sigma * (1.0 + preact * (1.0 - sigma))
        dhidden = (logit_grad[:, None] * out * slope).astype(bf16)
        term = lax.dot_general(dhidden, w, (((1,), (1,)), ((), ())), preferred_element_type=f32)
        dinputs = term if dinputs is None else dinputs + term
    return dinputs


def local(owners, local_rows, weights, labels, table, accum, w_in, b_in, w_out):
    samples, fields, bag_len = owners.shape
    table_rows, width = table.shape
    groups = lax.axis_size("owner")
    parts = lax.axis_size("dense")
    bags = samples * fields
    uniq = bags * bag_len // (2 * groups)
    padded = -(-uniq // lane) * lane

    def by_slot(x):
        return x.transpose(2, 1, 0).reshape(bag_len, bags)

    own, loc, w = by_slot(owners), by_slot(local_rows), by_slot(weights)
    distinct, distinct_row, named, spread = pl.pallas_call(
        functools.partial(distinct_body, table_rows),
        out_shape=(
            jax.ShapeDtypeStruct((uniq, 1), jnp.int32),
            jax.ShapeDtypeStruct((1, padded), jnp.int32),
            jax.ShapeDtypeStruct((groups, bags), jnp.int32),
            jax.ShapeDtypeStruct((groups, bags), f32),
        ),
        in_specs=[vmem()] * 3,
        out_specs=(vmem(),) * 4,
        name="distinct",
    )(own, loc, w)
    lists = pl.pallas_call(
        functools.partial(share_body, groups),
        out_shape=jax.ShapeDtypeStruct((groups, 1, padded), jnp.int32),
        in_specs=[vmem()],
        out_specs=vmem(),
        scratch_shapes=[
            pltpu.SemaphoreType.DMA((groups,)),
            pltpu.SemaphoreType.DMA((groups,)),
            pltpu.SemaphoreType.DMA,
        ],
        compiler_params=pltpu.CompilerParams(collective_id=0, has_side_effects=True),
        name="share",
    )(distinct_row).reshape(groups, padded)
    lists, w_later = lax.optimization_barrier((lists, w_in))
    pieces = head_pieces(w_later, b_in, w_out)
    depth = table_rows // 4
    found = pl.pallas_call(
        lookup_body,
        out_shape=jax.ShapeDtypeStruct((groups, uniq, width), bf16),
        in_specs=[vmem(), vmem()],
        out_specs=vmem(),
        scratch_shapes=[
            pltpu.VMEM((depth, 4 * width), bf16),
            pltpu.VMEM((padded, groups), jnp.int32),
        ],
        name="lookup",
    )(lists, table)
    rows = lax.all_to_all(found, "owner", split_axis=0, concat_axis=0, tiled=True)

    block = pl.BlockSpec((groups, samples), lambda f: (0, f))
    slots = pl.BlockSpec((bag_len, samples), lambda f: (0, f))
    field = pl.BlockSpec((samples, width), lambda f: (0, f))
    inputs = pl.pallas_call(
        pool_body,
        grid=(fields,),
        out_shape=jax.ShapeDtypeStruct((samples, fields * width), bf16),
        in_specs=[vmem(), vmem(), block, block],
        out_specs=field,
        name="pool",
    )(distinct_row[:, :uniq], rows, named, spread)

    dinputs = head(inputs, labels, pieces)

    grads, weight_grad = pl.pallas_call(
        backward_body,
        grid=(fields,),
        out_shape=(
            jax.ShapeDtypeStruct((groups, uniq, width), bf16),
            jax.ShapeDtypeStruct((bag_len, bags), f32),
        ),
        in_specs=[vmem(), vmem(), block, block, slots, slots, field],
        out_specs=(vmem(), slots),
        scratch_shapes=[
            pltpu.VMEM((groups, uniq, width), f32),
            pltpu.VMEM((uniq, samples), jnp.int32),
        ],
        name="backward",
    )(distinct, rows, named, spread, own, w, dinputs)
    weight_grad = weight_grad.reshape(bag_len, fields, samples).transpose(2, 1, 0)

    got = lax.all_to_all(grads, "owner", split_axis=0, concat_axis=0, tiled=True)
    chunk = table_rows // 2
    sums = []
    for base in range(0, table_rows, chunk):
        row_part = pl.pallas_call(
            functools.partial(collect_body, base),
            out_shape=jax.ShapeDtypeStruct((chunk, width), bf16),
            in_specs=[vmem(), vmem()],
            out_specs=vmem(),
            scratch_shapes=[
                pltpu.VMEM((padded, groups), jnp.int32),
                pltpu.VMEM((chunk // 2, 2 * width), f32),
            ],
            name="collect",
        )(lists, got)
        if parts == 2:
            other = lax.ppermute(row_part, "dense", [(0, 1), (1, 0)])
            sums.append(row_part.astype(f32) + other.astype(f32))
        else:
            sums.append(lax.psum(row_part, "dense").astype(f32))
    row_grad = jnp.concatenate(sums, axis=0)
    new_accum = accum + jnp.mean(row_grad * row_grad, axis=-1)
    new_table = table - step_size * row_grad / jnp.sqrt(new_accum)[:, None]
    return (new_table, new_accum, weight_grad)


def solution(mesh):
    placed = (
        P(("owner", "dense"), None, None),
        P(("owner", "dense"), None, None),
        P(("owner", "dense"), None, None),
        P(("owner", "dense")),
        P("owner", None),
        P("owner"),
        P(None, "dense"),
        P("dense"),
        P("dense"),
    )
    return jax.shard_map(
        local,
        mesh=mesh,
        in_specs=placed,
        out_specs=(P("owner", None), P("owner"), P(("owner", "dense"), None, None)),
        check_vma=False,
    )
```

```python
import functools

import jax
import jax.numpy as jnp
from jax import lax
from jax.experimental import pallas as pl
from jax.experimental.pallas import tpu as pltpu
from jax.sharding import PartitionSpec as P

step_size = 0.5
lane = 128
f32 = jnp.float32
bf16 = jnp.bfloat16


def vmem():
    return pl.BlockSpec(memory_space=pltpu.VMEM)


def distinct_body(table_rows, own_ref, loc_ref, w_ref, uniq_ref, row_ref, lo_ref, wo_ref):
    bag_len, bags = own_ref.shape
    groups = lo_ref.shape[0]
    uniq = uniq_ref.shape[0]
    padded = row_ref.shape[1]
    highs = table_rows // lane
    counts = jnp.zeros((highs, lane), f32)
    owner_at = lax.broadcasted_iota(jnp.int32, (groups, bags), 0)
    low_at = lax.broadcasted_iota(jnp.int32, (lane, bags), 0)
    high_at = lax.broadcasted_iota(jnp.int32, (highs, bags), 0)
    named = jnp.full((groups, bags), -1, jnp.int32)
    weight = jnp.zeros((groups, bags), f32)
    for slot in range(bag_len):
        loc = loc_ref[slot : slot + 1, :]
        hit = own_ref[slot : slot + 1, :] == owner_at
        named = jnp.where(hit, loc, named)
        weight = jnp.where(hit, w_ref[slot : slot + 1, :], weight)
        low = jnp.where(jnp.bitwise_and(loc, lane - 1) == low_at, 1.0, 0.0).astype(bf16)
        high = jnp.where(jnp.right_shift(loc, 7) == high_at, 1.0, 0.0).astype(bf16)
        counts += lax.dot_general(high, low, (((1,), (1,)), ((), ())), preferred_element_type=f32)
    lo_ref[...] = named
    wo_ref[...] = weight
    present = jnp.where(counts > 0.0, 1.0, 0.0)
    upper = jnp.where(
        lax.broadcasted_iota(jnp.int32, (lane, lane), 0)
        <= lax.broadcasted_iota(jnp.int32, (lane, lane), 1),
        1.0,
        0.0,
    ).astype(bf16)
    inclusive = jnp.dot(present.astype(bf16), upper, preferred_element_type=f32)
    place = lax.broadcasted_iota(jnp.int32, (padded, lane), 0).astype(f32)
    lane_at = lax.broadcasted_iota(jnp.int32, (1, lane), 1).astype(f32)
    before = jnp.zeros((1, 1), f32)
    found = jnp.where(place < float(uniq), 0.0, -1.0)
    for h in range(highs):
        here = present[h : h + 1, :]
        rank = jnp.where(here > 0.0, inclusive[h : h + 1, :] + before - 1.0, -1.0)
        found += jnp.where(place == rank, lane_at + float(h * lane), 0.0)
        before += jnp.sum(here, axis=1, keepdims=True)
    column = jnp.sum(found, axis=1, keepdims=True)
    uniq_ref[...] = column[:uniq].astype(jnp.int32)
    row_ref[...] = jnp.broadcast_to(column, (padded, lane)).T[0:1].astype(jnp.int32)


def share_body(groups, row_ref, out_ref, send_sem, recv_sem, own_sem):
    me = lax.axis_index("owner")
    barrier = pltpu.get_barrier_semaphore()
    for k in range(1, groups):
        peer = lax.rem(me + k, groups)
        pl.semaphore_signal(
            barrier, inc=1, device_id={"owner": peer}, device_id_type=pl.DeviceIdType.MESH
        )
    pl.semaphore_wait(barrier, groups - 1)
    copies = []
    for k in range(1, groups):
        copies.append(
            pltpu.make_async_remote_copy(
                src_ref=row_ref,
                dst_ref=out_ref.at[me],
                send_sem=send_sem.at[k],
                recv_sem=recv_sem.at[k],
                device_id={"owner": lax.rem(me + k, groups)},
                device_id_type=pl.DeviceIdType.MESH,
            )
        )
    for copy in copies:
        copy.start()
    mine = pltpu.make_async_copy(row_ref, out_ref.at[me], own_sem)
    mine.start()
    mine.wait()
    for copy in copies:
        copy.wait()


def lookup_body(list_ref, table_ref, out_ref, wide, columns):
    groups, uniq, width = out_ref.shape
    depth = wide.shape[0]
    folds = table_ref.shape[0] // depth
    for j in range(folds):
        wide[:, j * width : (j + 1) * width] = table_ref[j * depth : (j + 1) * depth, :].astype(bf16)
    columns[...] = list_ref[...].T
    at = lax.broadcasted_iota(jnp.int32, (uniq, depth), 1)
    for q in range(groups):
        ids = columns[:uniq, q : q + 1]
        fold = ids // depth
        pick = jnp.where(ids - fold * depth == at, 1.0, 0.0).astype(bf16)
        every = jnp.dot(pick, wide[...], preferred_element_type=f32)
        row = every[:, :width]
        for j in range(1, folds):
            row = jnp.where(fold == j, every[:, j * width : (j + 1) * width], row)
        out_ref[q] = row.astype(bf16)


def pool_body(uniq_ref, rows_ref, lo_ref, wo_ref, out_ref):
    groups = rows_ref.shape[0]
    named = lo_ref[...].T
    weight = wo_ref[...].T
    total = jnp.sum(weight, axis=1, keepdims=True)
    distinct = uniq_ref[...]
    acc = jnp.zeros(out_ref.shape, f32)
    for o in range(groups):
        mix = jnp.where(named[:, o : o + 1] == distinct, weight[:, o : o + 1], 0.0).astype(bf16)
        acc += jnp.dot(mix, rows_ref[o], preferred_element_type=f32)
    out_ref[...] = (acc / total).astype(bf16)


def backward_body(
    start, last, uniq_ref, rows_ref, lo_ref, wo_ref, own_ref, w_ref, dp_ref, before_ref,
    grad_ref, wg_ref, acc, wide
):
    groups, uniq, _ = grad_ref.shape
    f = pl.program_id(0)

    @pl.when(f == 0)
    def _():
        acc[...] = jnp.zeros_like(acc)
        wide[...] = jnp.broadcast_to(uniq_ref[start : start + uniq, :], wide.shape)

    dp = dp_ref[...]
    dp_rows = dp.astype(bf16)
    dp_cols = dp.T.astype(bf16)
    slot_w = w_ref[...]
    own = own_ref[...]
    total = jnp.sum(slot_w, axis=0, keepdims=True)
    scaled = wo_ref[...] / total
    along = before_ref[...]
    for o in range(groups):
        hit = wide[...] == lo_ref[o : o + 1, :]
        mix = jnp.where(hit, scaled[o : o + 1, :], 0.0).astype(bf16)
        acc[o] += jnp.dot(mix, dp_rows, preferred_element_type=f32)
        rows = rows_ref[o, start : start + uniq, :]
        dots = jnp.dot(rows, dp_cols, preferred_element_type=f32)
        mine = jnp.sum(jnp.where(hit, dots, 0.0), axis=0, keepdims=True)
        along += jnp.where(own == o, mine, 0.0)
    if last:
        centre = jnp.sum(slot_w * along, axis=0, keepdims=True) / total
        wg_ref[...] = (along - centre) / total
    else:
        wg_ref[...] = along

    @pl.when(f == pl.num_programs(0) - 1)
    def _():
        grad_ref[...] = acc[...].astype(bf16)


def collect_body(base, list_ref, *refs):
    *got_refs, out_ref, columns, acc = refs
    groups, _, width = got_refs[0].shape
    half = out_ref.shape[0] // 2
    columns[...] = list_ref[...].T - base
    acc[...] = jnp.zeros_like(acc)
    start = 0
    for got_ref in got_refs:
        uniq = got_ref.shape[1]
        at = lax.broadcasted_iota(jnp.int32, (half, uniq), 0)
        for q in range(groups):
            row = list_ref[q : q + 1, start : start + uniq] - base
            row = jnp.where(row >= half, row - half, row)
            pick = jnp.where(row == at, 1.0, 0.0).astype(bf16)
            ids = columns[start : start + uniq, q : q + 1]
            got = got_ref[q].astype(f32)
            first = jnp.where(ids < half, got, 0.0)
            second = jnp.where(ids >= half, got, 0.0)
            both = jnp.concatenate([first, second], axis=1).astype(bf16)
            acc[...] += jnp.dot(pick, both, preferred_element_type=f32)
        start += uniq
    out_ref[:half] = acc[:, :width].astype(bf16)
    out_ref[half:] = acc[:, width:].astype(bf16)


def send_weights(w_in, b_in, w_out):
    parts = lax.axis_size("dense")
    half = w_in.shape[1] // 2
    core = lax.rem(lax.axis_index("owner"), 2)
    mine = lax.dynamic_slice_in_dim(w_in, core * half, half, axis=1)
    arrived = []
    for shift in range(1, parts):
        ring = [(d, (d + shift) % parts) for d in range(parts)]
        arrived.append(tuple(lax.ppermute(x, "dense", ring) for x in (mine, b_in, w_out)))
    return arrived


def head_pieces(w_in, b_in, w_out, arrived):
    groups = lax.axis_size("owner")
    half = w_in.shape[1] // 2
    core = lax.rem(lax.axis_index("owner"), 2)
    swap = [(g, g + 1 - 2 * (g % 2)) for g in range(groups)]
    pieces = [(w_in, b_in, w_out)]
    for w_here, b_all, o_all in arrived:
        w_there = lax.ppermute(w_here, "owner", swap)
        for w_piece, at in ((w_here, core * half), (w_there, (1 - core) * half)):
            pieces.append(
                (
                    w_piece,
                    lax.dynamic_slice_in_dim(b_all, at, half),
                    lax.dynamic_slice_in_dim(o_all, at, half),
                )
            )
    return pieces


def head(inputs, labels, pieces):
    kept = []
    logits = jnp.zeros((inputs.shape[0],), f32)
    for w, b, out in pieces:
        out = out.astype(f32)
        preact = jnp.dot(inputs, w, preferred_element_type=f32) + b.astype(f32)
        sigma = jax.nn.sigmoid(preact)
        logits += jnp.sum(preact * sigma * out, axis=-1)
        kept.append((w, out, preact, sigma))
    logit_grad = jax.nn.sigmoid(logits) - labels.astype(f32)
    dinputs = None
    for w, out, preact, sigma in kept:
        slope = sigma * (1.0 + preact * (1.0 - sigma))
        dhidden = (logit_grad[:, None] * out * slope).astype(bf16)
        term = lax.dot_general(dhidden, w, (((1,), (1,)), ((), ())), preferred_element_type=f32)
        dinputs = term if dinputs is None else dinputs + term
    return dinputs


def local(owners, local_rows, weights, labels, table, accum, w_in, b_in, w_out):
    samples, fields, bag_len = owners.shape
    table_rows, width = table.shape
    groups = lax.axis_size("owner")
    parts = lax.axis_size("dense")
    bags = samples * fields
    uniq = bags * bag_len // (2 * groups)
    padded = -(-uniq // lane) * lane
    arrived = send_weights(w_in, b_in, w_out)

    def by_slot(x):
        return x.transpose(2, 1, 0).reshape(bag_len, bags)

    own, loc, w = by_slot(owners), by_slot(local_rows), by_slot(weights)
    distinct, distinct_row, named, spread = pl.pallas_call(
        functools.partial(distinct_body, table_rows),
        out_shape=(
            jax.ShapeDtypeStruct((uniq, 1), jnp.int32),
            jax.ShapeDtypeStruct((1, padded), jnp.int32),
            jax.ShapeDtypeStruct((groups, bags), jnp.int32),
            jax.ShapeDtypeStruct((groups, bags), f32),
        ),
        in_specs=[vmem()] * 3,
        out_specs=(vmem(),) * 4,
        name="distinct",
    )(own, loc, w)
    lists = pl.pallas_call(
        functools.partial(share_body, groups),
        out_shape=jax.ShapeDtypeStruct((groups, 1, padded), jnp.int32),
        in_specs=[vmem()],
        out_specs=vmem(),
        scratch_shapes=[
            pltpu.SemaphoreType.DMA((groups,)),
            pltpu.SemaphoreType.DMA((groups,)),
            pltpu.SemaphoreType.DMA,
        ],
        compiler_params=pltpu.CompilerParams(collective_id=0, has_side_effects=True),
        name="share",
    )(distinct_row).reshape(groups, padded)
    depth = table_rows // 4
    found = pl.pallas_call(
        lookup_body,
        out_shape=jax.ShapeDtypeStruct((groups, uniq, width), bf16),
        in_specs=[vmem(), vmem()],
        out_specs=vmem(),
        scratch_shapes=[
            pltpu.VMEM((depth, 4 * width), bf16),
            pltpu.VMEM((padded, groups), jnp.int32),
        ],
        name="lookup",
    )(lists, table)
    rows = lax.all_to_all(found, "owner", split_axis=0, concat_axis=0, tiled=True)

    block = pl.BlockSpec((groups, samples), lambda f: (0, f))
    slots = pl.BlockSpec((bag_len, samples), lambda f: (0, f))
    field = pl.BlockSpec((samples, width), lambda f: (0, f))
    inputs = pl.pallas_call(
        pool_body,
        grid=(fields,),
        out_shape=jax.ShapeDtypeStruct((samples, fields * width), bf16),
        in_specs=[vmem(), vmem(), block, block],
        out_specs=field,
        name="pool",
    )(distinct_row[:, :uniq], rows, named, spread)

    inputs, arrived = lax.optimization_barrier((inputs, arrived))
    pieces = head_pieces(w_in, b_in, w_out, arrived)
    dinputs = head(inputs, labels, pieces)

    spans = [(0, uniq)]
    weight_grad = jnp.zeros((bag_len, bags), f32)
    got = []
    for start, count in spans:
        last = start + count == uniq
        grads, weight_grad = pl.pallas_call(
            functools.partial(backward_body, start, last),
            grid=(fields,),
            out_shape=(
                jax.ShapeDtypeStruct((groups, count, width), bf16),
                jax.ShapeDtypeStruct((bag_len, bags), f32),
            ),
            in_specs=[vmem(), vmem(), block, block, slots, slots, field, slots],
            out_specs=(vmem(), slots),
            scratch_shapes=[
                pltpu.VMEM((groups, count, width), f32),
                pltpu.VMEM((count, samples), jnp.int32),
            ],
            name="backward",
            cost_estimate=pl.CostEstimate(
                flops=4 * groups * count * width * bags,
                bytes_accessed=4 * groups * count * width,
                transcendentals=0,
            ),
        )(distinct, rows, named, spread, own, w, dinputs, weight_grad)
        got.append(lax.all_to_all(grads, "owner", split_axis=0, concat_axis=0, tiled=True))
    weight_grad = weight_grad.reshape(bag_len, fields, samples).transpose(2, 1, 0)

    chunk = table_rows // 2
    sums = []
    for base in range(0, table_rows, chunk):
        row_part = pl.pallas_call(
            functools.partial(collect_body, base),
            out_shape=jax.ShapeDtypeStruct((chunk, width), bf16),
            in_specs=[vmem()] * (1 + len(got)),
            out_specs=vmem(),
            scratch_shapes=[
                pltpu.VMEM((padded, groups), jnp.int32),
                pltpu.VMEM((chunk // 2, 2 * width), f32),
            ],
            name="collect",
        )(lists, *got)
        if parts == 2:
            other = lax.ppermute(row_part, "dense", [(0, 1), (1, 0)])
            sums.append(row_part.astype(f32) + other.astype(f32))
        else:
            sums.append(lax.psum(row_part, "dense").astype(f32))
    row_grad = jnp.concatenate(sums, axis=0)
    new_accum = accum + jnp.mean(row_grad * row_grad, axis=-1)
    new_table = table - step_size * row_grad / jnp.sqrt(new_accum)[:, None]
    return (new_table, new_accum, weight_grad)


def solution(mesh):
    placed = (
        P(("owner", "dense"), None, None),
        P(("owner", "dense"), None, None),
        P(("owner", "dense"), None, None),
        P(("owner", "dense")),
        P("owner", None),
        P("owner"),
        P(None, "dense"),
        P("dense"),
        P("dense"),
    )
    return jax.shard_map(
        local,
        mesh=mesh,
        in_specs=placed,
        out_specs=(P("owner", None), P("owner"), P(("owner", "dense"), None, None)),
        check_vma=False,
    )
```
